32 devices in a mesh: rows: 8 (over z, y), band: 4 (over x, core).
Axes of the slice: x: 2, y: 2, z: 4, core: 2. Of those that a mesh axis runs over, the one named last changes fastest.
Arguments:
- coupling: bfloat16 [16384, 2560], P('rows', 'band'), may hold values from -1 to 2
- sketch: bfloat16 [16384, 256], P('rows'), may hold values from -256 to 256
Outputs:
- basis_out: bfloat16 [16384, 256], P(('rows', 'band'))
- factor: float32 [256, 256], replicated
The draws below stay inside these ranges and needn't reach their ends.
All inputs are finite; a program needn't handle non-finite values.
Results may differ from the reference program's by a relative error of at most 0.015.
Values may be sent and summed in bfloat16 or wider, within the bound.
No kernel may reach another device: no remote copies, remote signals or barrier semaphores. Data moves between devices by JAX's collectives and lax.ppermute only.
A program may use at most 256 MiB of HBM per device.

```python
import math
import jax
import jax.numpy as jnp
from jax import lax

K = 256
HB = 1024
TB = 512
N = 16384
N_BAND = 4


def draw_coupling(key, part):
    shape_all = (N, TB + 2 * HB)
    row_ids = lax.broadcasted_iota(jnp.int32, shape_all, 0)
    col_ids = lax.broadcasted_iota(jnp.int32, shape_all, 1)
    on_diagonal = col_ids == row_ids % TB + HB
    key_noise = jax.random.fold_in(key, 11)
    key_diag = jax.random.fold_in(key, 12)
    key_rows = jax.random.fold_in(key, 13)
    noise = jax.random.truncated_normal(key_noise, -4.0, 4.0, shape_all, jnp.float32)
    row_factor = jax.random.uniform(key_rows, (N, 1), jnp.float32, 0.5, 2.0)
    spread = 0.3 / math.sqrt(TB + 2 * HB)
    diag_values = jax.random.uniform(key_diag, (N, 1), jnp.float32, 0.75, 1.5)
    result = jnp.where(on_diagonal, diag_values, 0.0) + noise * spread * row_factor
    return result.astype(jnp.bfloat16)


def draw_sketch(key, part):
    key_noise = jax.random.fold_in(key, 21)
    key_rows = jax.random.fold_in(key, 22)
    position = lax.broadcasted_iota(jnp.float32, (N, 1), 0)
    ramp = 1.0 + 2.0 * position / (N - 1)
    noise = jax.random.truncated_normal(key_noise, -4.0, 4.0, (N, K), jnp.float32)
    row_scale = jnp.exp(jax.random.uniform(key_rows, (N, 1), jnp.float32, 0.0, math.log(8.0)))
    return (noise * row_scale * ramp).astype(jnp.bfloat16)


def setup_inputs(seed: int = 0) -> dict:
    key_list = jax.random.split(jax.random.key(seed), 3)
    coupling = draw_coupling(jax.random.fold_in(key_list[2], 71), 0)
    sketch = draw_sketch(jax.random.fold_in(key_list[2], 71), 0)
    return dict(coupling=coupling, sketch=sketch)


def cholesky_upper(gram):
    size = gram.shape[0]
    positions = jnp.arange(size, dtype=jnp.int32)

    def step(index, carry):
        work, upper = carry
        work_row = lax.dynamic_index_in_dim(work, index, 0, keepdims=False)
        pivot = jnp.sqrt(lax.dynamic_index_in_dim(work_row, index, 0, keepdims=False))
        row_now = jnp.where(positions >= index, work_row / pivot, jnp.zeros_like(work_row))
        upper = lax.dynamic_update_slice_in_dim(upper, row_now[None, :], index, 0)
        work = work - row_now[:, None] * row_now[None, :]
        return (work, upper)
    start = (gram, jnp.zeros_like(gram))
    return lax.fori_loop(0, size, step, start)[1]

def invert_upper(upper):
    size = upper.shape[0]
    positions = jnp.arange(size, dtype=jnp.int32)

    def step(count, solved):
        index = size - 1 - count
        upper_row = lax.dynamic_index_in_dim(upper, index, 0, keepdims=False)
        pivot = lax.dynamic_index_in_dim(upper_row, index, 0, keepdims=False)
        unit_row = jnp.where(positions == index, jnp.ones_like(upper_row), jnp.zeros_like(upper_row))
        row_now = (unit_row - jnp.dot(upper_row, solved, precision=lax.Precision.HIGHEST)) / pivot
        return lax.dynamic_update_slice_in_dim(solved, row_now[None, :], index, 0)
    return lax.fori_loop(0, size, step, jnp.zeros_like(upper))

def apply_band(coupling, field):
    padded = jnp.pad(field, ((HB, HB), (0, 0)))
    width_dev = (TB + 2 * HB) // N_BAND

    def one_tile(tile_index):
        start_row = (tile_index * TB).astype(jnp.int32)
        block_rows = lax.dynamic_slice_in_dim(coupling, start_row, TB, 0).astype(jnp.float32)
        block_rows = block_rows.reshape(TB, N_BAND, width_dev)
        window = lax.dynamic_slice_in_dim(padded, start_row, TB + 2 * HB, 0).astype(jnp.float32)
        window = window.reshape(N_BAND, width_dev, K)
        group_sums = jnp.einsum('ibw,bwk->bik', block_rows, window)
        rounded = lax.optimization_barrier(group_sums.astype(jnp.bfloat16))
        return lax.optimization_barrier(jnp.sum(rounded.astype(jnp.float32), axis=0))
    result = lax.map(one_tile, jnp.arange(N // TB, dtype=jnp.int32))
    return result.reshape(N, K)

def reference(coupling, sketch):
    first_pass = apply_band(coupling, sketch).astype(jnp.bfloat16)
    second = apply_band(coupling, first_pass)
    gram_matrix = jnp.dot(second.T, second, precision=lax.Precision.HIGHEST, preferred_element_type=jnp.float32)
    upper_factor = cholesky_upper(gram_matrix)
    inverse = invert_upper(upper_factor)
    scale_root = math.sqrt(N)
    basis_out = (jnp.dot(second, inverse, precision=lax.Precision.HIGHEST, preferred_element_type=jnp.float32) * scale_root).astype(jnp.bfloat16)
    factor = upper_factor / scale_root
    return (basis_out, factor)
```

```python
import functools
import math

import jax
import jax.numpy as jnp
from jax import lax
from jax.experimental import pallas as pl
from jax.experimental.pallas import tpu as pltpu
from jax.sharding import PartitionSpec as P

HB = 1024
TB = 512
HIGHEST = lax.Precision.HIGHEST
F32 = jnp.float32
BF16 = jnp.bfloat16
NB = 64
PIV = 8
VMEM = pl.BlockSpec(memory_space=pltpu.VMEM)
ANY = pl.BlockSpec(memory_space=pl.ANY)


def flip(array, axis, bit):
    count = lax.axis_size(axis)
    return lax.ppermute(array, axis, [(i, i ^ bit) for i in range(count)])


def two_tiles(base, coupling, field_ref, fetched, sems, keep_ref, send_ref):
    width = coupling.shape[1]
    band = lax.axis_index("band")
    half, core = band // 2, band % 2
    copies = []
    for slot in range(2):
        tile = core if slot == 1 else 1 - core
        rows = pl.ds(pl.multiple_of(base + tile * TB, TB), TB)
        copies.append(
            pltpu.make_async_copy(coupling.at[rows, :], fetched.at[slot], sems.at[slot])
        )
    return copies, (band, half, core, width)


def run_tiles(copies, place, field_ref, fetched, keep_ref, send_ref):
    band, half, core, width = place
    for slot, out in ((0, send_ref), (1, keep_ref)):
        tile = core if slot == 1 else 1 - core
        first = pl.multiple_of(tile * TB + band * width - half * HB, 128)
        copies[slot].wait()
        out[...] = jnp.dot(
            fetched[slot], field_ref[pl.ds(first, width), :], preferred_element_type=F32
        ).astype(BF16)


def early_kernel(coupling, field, keep_ref, send_ref, fetched, sems):
    half = lax.axis_index("band") // 2
    copies, place = two_tiles((1 - half) * HB, coupling, field, fetched, sems, keep_ref, send_ref)
    for copy in copies:
        copy.start()
    run_tiles(copies, place, field, fetched, keep_ref, send_ref)


def early_kernel_tiles(coupling, own, own2, far, far2, keep_ref, send_ref, field, fetched, sems):
    band = lax.axis_index("band")
    half, core = band // 2, band % 2
    copies, place = two_tiles((1 - half) * HB, coupling, field, fetched, sems, keep_ref, send_ref)
    for copy in copies:
        copy.start()
    for ref, tile in (
        (own, 2 * half + core),
        (own2, 2 * half + 1 - core),
        (far, 2 * (1 - half) + core),
        (far2, 2 * (1 - half) + 1 - core),
    ):
        field[pl.ds(pl.multiple_of(tile * TB, TB), TB), :] = ref[...]
    run_tiles(copies, place, field, fetched, keep_ref, send_ref)


def late_kernel(coupling, near0, near1, halo, halo2, keep_ref, send_ref, field, fetched, sems):
    band = lax.axis_index("band")
    half, core = band // 2, band % 2
    copies, place = two_tiles(half * HB, coupling, field, fetched, sems, keep_ref, send_ref)
    for copy in copies:
        copy.start()
    near_at, halo_at = (1 - half) * HB, half * HB
    for ref, first in (
        (near0, near_at + core * TB),
        (near1, near_at + (1 - core) * TB),
        (halo, halo_at + core * TB),
        (halo2, halo_at + (1 - core) * TB),
    ):
        field[pl.ds(pl.multiple_of(first, TB), TB), :] = ref[...]
    run_tiles(copies, place, field, fetched, keep_ref, send_ref)


def late_kernel_slab(coupling, slab, halo, halo2, keep_ref, send_ref, field, fetched, sems):
    band = lax.axis_index("band")
    half, core = band // 2, band % 2
    copies, place = two_tiles(half * HB, coupling, field, fetched, sems, keep_ref, send_ref)
    for copy in copies:
        copy.start()
    near_at, halo_at = pl.multiple_of((1 - half) * HB, HB), half * HB
    field[pl.ds(near_at, HB), :] = slab[pl.ds(pl.multiple_of(half * HB, HB), HB), :]
    for ref, first in ((halo, halo_at + core * TB), (halo2, halo_at + (1 - core) * TB)):
        field[pl.ds(pl.multiple_of(first, TB), TB), :] = ref[...]
    run_tiles(copies, place, field, fetched, keep_ref, send_ref)


def product(kernel, coupling, *fields):
    width, columns = coupling.shape[1], fields[0].shape[1]
    scratch = [pltpu.VMEM((2, TB, width), BF16), pltpu.SemaphoreType.DMA((2,))]
    if kernel is not early_kernel:
        scratch = [pltpu.VMEM((2 * HB, columns), BF16)] + scratch
    tile = jax.ShapeDtypeStruct((TB, columns), BF16)
    return pl.pallas_call(
        kernel,
        out_shape=(tile, tile),
        in_specs=[ANY] + [VMEM] * len(fields),
        out_specs=(VMEM, VMEM),
        scratch_shapes=scratch,
        name=kernel.__name__,
        cost_estimate=pl.CostEstimate(
            flops=4 * TB * width * columns, bytes_accessed=4 * TB * width, transcendentals=0
        ),
    )(coupling, *fields)


def gram_kernel(keep, near, far, second_ref, mine_ref, other_ref, packed):
    core = lax.axis_index("band") % 2
    second = keep[...].astype(F32) + near[...].astype(F32) + far[...].astype(F32)
    second_ref[...] = second
    size = second.shape[1]
    mid = size // 2
    over_rows = (((0,), (0,)), ((), ()))
    top = lax.dot_general(
        second[:, :mid], second, over_rows, precision=HIGHEST, preferred_element_type=F32
    )
    low = lax.dot_general(
        second[:, mid:], second[:, mid:], over_rows, precision=HIGHEST, preferred_element_type=F32
    )
    packed[0:mid, :] = top[:, :mid]
    packed[mid:size, :] = top[:, mid:]
    packed[size:, :] = low
    part = 3 * mid // 2
    mine_ref[...] = packed[pl.ds(pl.multiple_of(core * part, 64), part), :]
    other_ref[...] = packed[pl.ds(pl.multiple_of((1 - core) * part, 64), part), :]


def gram(keep, near, far):
    rows, size = keep.shape
    part = jax.ShapeDtypeStruct((3 * size // 4, size // 2), F32)
    return pl.pallas_call(
        gram_kernel,
        out_shape=(jax.ShapeDtypeStruct((rows, size), F32), part, part),
        in_specs=[VMEM] * 3,
        out_specs=(VMEM,) * 3,
        scratch_shapes=[pltpu.VMEM((3 * size // 2, size // 2), F32)],
        name="gram_kernel",
    )(keep, near, far)


def factor_block(block):
    size = block.shape[0]
    groups = size // 8
    rows = [block[8 * i : 8 * i + 8, :] for i in range(groups)]
    shape = rows[0].shape
    sub = lax.broadcasted_iota(jnp.int32, shape, 0)
    for first in range(0, size, PIV):
        own, at = first // 8, first % 8
        pivots = range(PIV)
        row = [jnp.broadcast_to(rows[own][at + p : at + p + 1, :], shape) for p in pivots]
        column = [
            {
                q: jnp.broadcast_to(rows[q][:, first + p : first + p + 1], shape)
                for q in range(own, groups)
            }
            for p in pivots
        ]
        entry = {
            (p, t): jnp.broadcast_to(column[p][own][at + t : at + t + 1, :], shape)
            for p in pivots
            for t in range(p, PIV)
        }
        upper, scale = {}, []
        for p in pivots:
            scale.append(lax.rsqrt(entry[p, p]))
            for t in range(p + 1, PIV):
                upper[p, t] = entry[p, t] * scale[p]
            for t in range(p + 1, PIV):
                for w in range(t, PIV):
                    entry[t, w] = entry[t, w] - upper[p, t] * upper[p, w]

        def solve(values):
            values = list(values)
            for p in pivots:
                values[p] = values[p] * scale[p]
                for t in range(p + 1, PIV):
                    values[t] = values[t] - upper[p, t] * values[p]
            return values

        done = solve(row)
        for q in range(own, groups):
            new = rows[q]
            if PIV < 8 or q > own:
                weight = solve([column[p][q] for p in pivots])
                total = weight[0] * done[0]
                for p in range(1, PIV):
                    total = total + weight[p] * done[p]
                new = new - total
            if q == own:
                new = jnp.where(sub >= at + PIV, new, rows[q])
                for p in pivots:
                    new = jnp.where(sub == at + p, done[p], new)
            rows[q] = new
    return jnp.concatenate(rows, 0)


def factor_kernel(scale_root, mine, other, second, basis_ref, factor_ref, a_ref, b_ref, packed):
    core = lax.axis_index("band") % 2
    part, mid = mine.shape
    size = 2 * mid
    packed[pl.ds(pl.multiple_of(core * part, 64), part), :] = mine[...]
    packed[pl.ds(pl.multiple_of((1 - core) * part, 64), part), :] = other[...]
    a_ref[0:mid, 0:mid] = packed[0:mid, :]
    a_ref[0:mid, mid:size] = packed[mid:size, :]
    a_ref[mid:size, mid:size] = packed[size:, :]
    a_ref[mid:size, 0:mid] = jnp.zeros((mid, mid), F32)
    row_id = lax.broadcasted_iota(jnp.int32, (size, size), 0)
    col_id = lax.broadcasted_iota(jnp.int32, (size, size), 1)
    b_ref[...] = jnp.where(row_id == col_id, 1.0, 0.0).astype(F32)
    factor_ref[...] = jnp.zeros_like(factor_ref)
    lane = lax.broadcasted_iota(jnp.int32, (NB, 128), 1)
    row = lax.broadcasted_iota(jnp.int32, (NB, 128), 0)
    over_rows = (((0,), (0,)), ((), ()))
    for first in range(0, size, NB):
        after = first + NB
        low = (first // 128) * 128
        shift = first - low
        block = a_ref[first:after, low : low + 128]
        if shift:
            block = pltpu.roll(block, 128 - shift, 1)
        block = jnp.where(lane < NB, block, jnp.where(lane - NB == row, 1.0, 0.0))
        block = factor_block(block)
        diagonal = jnp.where((lane < NB) & (lane >= row), block, 0.0)
        if shift:
            diagonal = pltpu.roll(diagonal, shift, 1)
        solve = jnp.where(lane <= row, pltpu.roll(block, 128 - NB, 1), 0.0)[:, :NB]
        high = low + 128
        right = jnp.dot(
            solve, a_ref[first:after, low:size], precision=HIGHEST, preferred_element_type=F32
        )
        column = lax.broadcasted_iota(jnp.int32, right.shape, 1) + low
        right = jnp.where(column >= after, right, 0.0)
        left = jnp.dot(
            solve, b_ref[first:after, 0:high], precision=HIGHEST, preferred_element_type=F32
        )
        if size > high:
            diagonal = jnp.concatenate([diagonal, jnp.zeros((NB, size - high), F32)], 1)
        factor_ref[first:after, low:size] = (right + diagonal) * (1.0 / scale_root)
        b_ref[first:after, 0:high] = left
        if after < size:
            edge = (after // 128) * 128
            ahead = right[:, edge - low :]
            on_a = lax.dot_general(
                ahead, ahead, over_rows, precision=HIGHEST, preferred_element_type=F32
            )
            on_b = lax.dot_general(
                ahead, left, over_rows, precision=HIGHEST, preferred_element_type=F32
            )
            skip = after - edge
            a_ref[after:size, edge:size] -= on_a[skip:, :]
            b_ref[after:size, 0:high] -= on_b[skip:, :]
    basis = lax.dot_general(
        second[...],
        b_ref[...],
        (((1,), (1,)), ((), ())),
        precision=HIGHEST,
        preferred_element_type=F32,
    )
    basis_ref[...] = (basis * scale_root).astype(BF16)


def factor_and_basis(mine, other, second, scale_root):
    rows, size = second.shape
    return pl.pallas_call(
        functools.partial(factor_kernel, scale_root),
        out_shape=(
            jax.ShapeDtypeStruct((rows, size), BF16),
            jax.ShapeDtypeStruct((size, size), F32),
        ),
        in_specs=[VMEM] * 3,
        out_specs=(VMEM, VMEM),
        scratch_shapes=[
            pltpu.VMEM((size, size), F32),
            pltpu.VMEM((size, size), F32),
            pltpu.VMEM((3 * size // 2, size // 2), F32),
        ],
        name="factor_kernel",
    )(mine, other, second)


def halo_step(send):
    slabs, bands = lax.axis_size("rows"), lax.axis_size("band")
    pairs = []
    for r in range(slabs):
        for b in range(bands):
            target = r + 1 if b < bands // 2 else r - 1
            if 0 <= target < slabs:
                pairs.append((r * bands + b, target * bands + b))
    return lax.ppermute(send, ("rows", "band"), pairs)


def inner_step(halo):
    return lax.ppermute(halo, "band", [(1, 0), (2, 3)])


def add16(*parts):
    total = parts[0].astype(F32)
    for part in parts[1:]:
        total = total + part.astype(F32)
    return total.astype(BF16)


def per_device(coupling, sketch):
    slabs = lax.axis_size("rows")
    band = lax.axis_index("band")
    half, core = band // 2, band % 2
    scale_root = math.sqrt(sketch.shape[0] * slabs)

    halo = halo_step(lax.dynamic_slice_in_dim(sketch, (1 - half) * HB + core * TB, TB, 0))
    keep, send = product(early_kernel, coupling, sketch)
    far = flip(add16(keep, flip(send, "band", 1)), "band", 2)
    halo2 = inner_step(halo)
    keep, send = product(late_kernel_slab, coupling, sketch, halo, halo2)
    own = add16(keep, flip(send, "band", 1), far)

    across = flip(own, "band", 2)
    own2 = flip(own, "band", 1)
    halo = halo_step(across)
    across2 = flip(across, "band", 1)
    keep, send = product(early_kernel_tiles, coupling, own, own2, across, across2)
    far = flip(add16(keep, flip(send, "band", 1)), "band", 2)
    halo2 = inner_step(halo)
    keep, send = product(late_kernel, coupling, own, own2, halo, halo2)
    near = flip(send, "band", 1)

    second, mine, other = gram(keep, near, far)
    mine = mine + flip(other, "band", 1)
    mine = mine + flip(mine, "band", 2)
    bit = 1
    while bit < slabs:
        mine = mine + flip(mine, "rows", bit)
        bit *= 2
    other = flip(mine, "band", 1)
    return factor_and_basis(mine, other, second, scale_root)


def solution(mesh):
    in_specs = (P("rows", "band"), P("rows", None))
    out_specs = (P(("rows", "band"), None), P())
    return jax.shard_map(
        per_device, mesh=mesh, in_specs=in_specs, out_specs=out_specs, check_vma=False
    )
```

```python
import functools
import math

import jax
import jax.numpy as jnp
from jax import lax
from jax.experimental import pallas as pl
from jax.experimental.pallas import tpu as pltpu
from jax.sharding import PartitionSpec as P


HB = 1024
TB = 512
HIGHEST = lax.Precision.HIGHEST
F32 = jnp.float32
BF16 = jnp.bfloat16
NB = 64
PIV = 8
VMEM = pl.BlockSpec(memory_space=pltpu.VMEM)
IN_HBM = pl.BlockSpec(memory_space=pltpu.HBM)


def flip(array, axis, bit):
    count = lax.axis_size(axis)
    return lax.ppermute(array, axis, [(i, i ^ bit) for i in range(count)])


def place():
    band = lax.axis_index("band")
    return band, band // 2, band % 2


def tile_rows(base, tile):
    return pl.ds(pl.multiple_of(base + tile * TB, TB), TB)


def run_tiles(base, coupling, field, keep_ref, send_ref):
    band, half, core = place()
    width = coupling.shape[1]
    for tile, out in ((1 - core, send_ref), (core, keep_ref)):
        first = pl.multiple_of(tile * TB + band * width - half * HB, 128)
        out[...] = jnp.dot(
            coupling[tile_rows(base, tile), :],
            field[pl.ds(first, width), :],
            preferred_element_type=F32,
        ).astype(BF16)


def first_kernel(coupling, slab, keep_ref, send_ref, edge_ref, coupling_ref, slab_ref, sems):
    _, half, core = place()
    base = pl.multiple_of((1 - half) * HB, HB)
    late = pl.multiple_of(half * HB, HB)
    loads = [pltpu.make_async_copy(slab, slab_ref, sems.at[0])]
    for slot, start in ((1, base), (2, late)):
        rows = pl.ds(start, HB)
        loads.append(
            pltpu.make_async_copy(coupling.at[rows, :], coupling_ref.at[rows, :], sems.at[slot])
        )
    for load in loads:
        load.start()
    loads[0].wait()
    edge_ref[...] = slab_ref[tile_rows(base, core), :]
    loads[1].wait()
    run_tiles(base, coupling_ref, slab_ref, keep_ref, send_ref)
    loads[2].wait()


def early_kernel(coupling, own, own2, far, far2, keep_ref, send_ref, field):
    _, half, core = place()
    for ref, tile in (
        (own, 2 * half + core),
        (own2, 2 * half + 1 - core),
        (far, 2 * (1 - half) + core),
        (far2, 2 * (1 - half) + 1 - core),
    ):
        field[tile_rows(0, tile), :] = ref[...]
    run_tiles((1 - half) * HB, coupling, field, keep_ref, send_ref)


def late_kernel(coupling, near0, near1, halo, halo2, keep_ref, send_ref, field):
    _, half, core = place()
    near_at, halo_at = (1 - half) * HB, half * HB
    for ref, start, tile in (
        (near0, near_at, core),
        (near1, near_at, 1 - core),
        (halo, halo_at, core),
        (halo2, halo_at, 1 - core),
    ):
        field[tile_rows(start, tile), :] = ref[...]
    run_tiles(half * HB, coupling, field, keep_ref, send_ref)


def late_kernel_slab(coupling, slab, halo, halo2, keep_ref, send_ref, field):
    _, half, core = place()
    near_at, halo_at = pl.multiple_of((1 - half) * HB, HB), half * HB
    field[pl.ds(near_at, HB), :] = slab[pl.ds(pl.multiple_of(half * HB, HB), HB), :]
    for ref, tile in ((halo, core), (halo2, 1 - core)):
        field[tile_rows(halo_at, tile), :] = ref[...]
    run_tiles(half * HB, coupling, field, keep_ref, send_ref)


def product(kernel, coupling, *fields):
    width, columns = coupling.shape[1], fields[0].shape[1]
    first = kernel is first_kernel
    outputs = [jax.ShapeDtypeStruct((TB, columns), BF16)] * 2
    scratch = [pltpu.VMEM((2 * HB, columns), BF16)]
    if first:
        outputs += [outputs[0]] + [
            jax.ShapeDtypeStruct(array.shape, BF16) for array in (coupling, fields[0])
        ]
        scratch = [pltpu.SemaphoreType.DMA((3,))]
    operands = (coupling, *fields)
    if first:
        operands = [pltpu.with_memory_space_constraint(array, pltpu.HBM) for array in operands]
    return pl.pallas_call(
        kernel,
        out_shape=outputs,
        in_specs=[IN_HBM] * 2 if first else [VMEM] * (1 + len(fields)),
        out_specs=[VMEM] * len(outputs),
        scratch_shapes=scratch,
        compiler_params=pltpu.CompilerParams(vmem_limit_bytes=8 << 20),
        cost_estimate=pl.CostEstimate(
            flops=4 * TB * width * columns, bytes_accessed=4 * TB * width, transcendentals=0
        ),
    )(*operands)


def gram_kernel(keep, near, far, second_ref, mine_ref, other_ref, packed):
    core = lax.axis_index("band") % 2
    second = keep[...].astype(F32) + near[...].astype(F32) + far[...].astype(F32)
    second_ref[...] = second
    size = second.shape[1]
    mid = size // 2
    over_rows = (((0,), (0,)), ((), ()))
    top = lax.dot_general(
        second[:, :mid], second, over_rows, precision=HIGHEST, preferred_element_type=F32
    )
    low = lax.dot_general(
        second[:, mid:], second[:, mid:], over_rows, precision=HIGHEST, preferred_element_type=F32
    )
    row = lax.broadcasted_iota(jnp.int32, (mid, mid), 0)
    column = lax.broadcasted_iota(jnp.int32, (mid, mid), 1)
    packed[0:mid, :] = top[:, mid:]
    packed[mid:size, :] = jnp.where(column >= row, top[:, :mid], low)
    diagonal = jnp.sum(jnp.where(column == row, low, 0.0), axis=0, keepdims=True)
    packed[size:, :] = jnp.broadcast_to(diagonal, (16, mid))
    part = mid + 8
    mine_ref[...] = packed[pl.ds(pl.multiple_of(core * part, 8), part), :]
    other_ref[...] = packed[pl.ds(pl.multiple_of((1 - core) * part, 8), part), :]


def gram(keep, near, far):
    rows, size = keep.shape
    part = jax.ShapeDtypeStruct((size // 2 + 8, size // 2), F32)
    return pl.pallas_call(
        gram_kernel,
        out_shape=(jax.ShapeDtypeStruct((rows, size), F32), part, part),
        in_specs=[VMEM] * 3,
        out_specs=(VMEM,) * 3,
        scratch_shapes=[pltpu.VMEM((size + 16, size // 2), F32)],
        name="gram_kernel",
        compiler_params=pltpu.CompilerParams(vmem_limit_bytes=12 << 20),
    )(keep, near, far)


def factor_block(block):
    size = block.shape[0]
    groups = size // 8
    rows = [block[8 * i : 8 * i + 8, :] for i in range(groups)]
    shape = rows[0].shape
    sub = lax.broadcasted_iota(jnp.int32, shape, 0)
    for first in range(0, size, PIV):
        own, at = first // 8, first % 8
        pivots = range(PIV)
        row = [jnp.broadcast_to(rows[own][at + p : at + p + 1, :], shape) for p in pivots]
        column = [
            {
                q: jnp.broadcast_to(rows[q][:, first + p : first + p + 1], shape)
                for q in range(own, groups)
            }
            for p in pivots
        ]
        entry = {
            (p, t): jnp.broadcast_to(column[p][own][at + t : at + t + 1, :], shape)
            for p in pivots
            for t in range(p, PIV)
        }
        upper, scale = {}, []
        for p in pivots:
            scale.append(lax.rsqrt(entry[p, p]))
            for t in range(p + 1, PIV):
                upper[p, t] = entry[p, t] * scale[p]
            for t in range(p + 1, PIV):
                for w in range(t, PIV):
                    entry[t, w] = entry[t, w] - upper[p, t] * upper[p, w]

        def solve(values):
            values = list(values)
            for p in pivots:
                values[p] = values[p] * scale[p]
                for t in range(p + 1, PIV):
                    values[t] = values[t] - upper[p, t] * values[p]
            return values

        done = solve(row)
        for q in range(own, groups):
            new = rows[q]
            if PIV < 8 or q > own:
                weight = solve([column[p][q] for p in pivots])
                total = weight[0] * done[0]
                for p in range(1, PIV):
                    total = total + weight[p] * done[p]
                new = new - total
            if q == own:
                new = jnp.where(sub >= at + PIV, new, rows[q])
                for p in pivots:
                    new = jnp.where(sub == at + p, done[p], new)
            rows[q] = new
    return jnp.concatenate(rows, 0)


def factor_kernel(scale_root, mine, other, second, basis_ref, factor_ref, a_ref, b_ref, packed):
    core = lax.axis_index("band") % 2
    part, mid = mine.shape
    size = 2 * mid
    packed[pl.ds(pl.multiple_of(core * part, 8), part), :] = mine[...]
    packed[pl.ds(pl.multiple_of((1 - core) * part, 8), part), :] = other[...]
    folded = packed[mid:size, :]
    turned = folded.T
    row = lax.broadcasted_iota(jnp.int32, (mid, mid), 0)
    column = lax.broadcasted_iota(jnp.int32, (mid, mid), 1)
    a_ref[0:mid, 0:mid] = jnp.where(column >= row, folded, turned)
    a_ref[0:mid, mid:size] = packed[0:mid, :]
    diagonal = jnp.broadcast_to(packed[size : size + 1, :], (mid, mid))
    a_ref[mid:size, mid:size] = jnp.where(
        column < row, folded, jnp.where(column > row, turned, diagonal)
    )
    a_ref[mid:size, 0:mid] = jnp.zeros((mid, mid), F32)
    row_id = lax.broadcasted_iota(jnp.int32, (size, size), 0)
    col_id = lax.broadcasted_iota(jnp.int32, (size, size), 1)
    b_ref[...] = jnp.where(row_id == col_id, 1.0, 0.0).astype(F32)
    factor_ref[...] = jnp.zeros_like(factor_ref)
    lane = lax.broadcasted_iota(jnp.int32, (NB, 128), 1)
    row = lax.broadcasted_iota(jnp.int32, (NB, 128), 0)
    over_rows = (((0,), (0,)), ((), ()))
    for first in range(0, size, NB):
        after = first + NB
        low = (first // 128) * 128
        shift = first - low
        block = a_ref[first:after, low : low + 128]
        if shift:
            block = pltpu.roll(block, 128 - shift, 1)
        block = jnp.where(lane < NB, block, jnp.where(lane - NB == row, 1.0, 0.0))
        block = factor_block(block)
        diagonal = jnp.where((lane < NB) & (lane >= row), block, 0.0)
        if shift:
            diagonal = pltpu.roll(diagonal, shift, 1)
        solve = jnp.where(lane <= row, pltpu.roll(block, 128 - NB, 1), 0.0)[:, :NB]
        high = low + 128
        right = jnp.dot(
            solve, a_ref[first:after, low:size], precision=HIGHEST, preferred_element_type=F32
        )
        column = lax.broadcasted_iota(jnp.int32, right.shape, 1) + low
        right = jnp.where(column >= after, right, 0.0)
        left = jnp.dot(
            solve, b_ref[first:after, 0:high], precision=HIGHEST, preferred_element_type=F32
        )
        if size > high:
            diagonal = jnp.concatenate([diagonal, jnp.zeros((NB, size - high), F32)], 1)
        factor_ref[first:after, low:size] = (right + diagonal) * (1.0 / scale_root)
        b_ref[first:after, 0:high] = left
        if after < size:
            edge = (after // 128) * 128
            ahead = right[:, edge - low :]
            on_a = lax.dot_general(
                ahead, ahead, over_rows, precision=HIGHEST, preferred_element_type=F32
            )
            on_b = lax.dot_general(
                ahead, left, over_rows, precision=HIGHEST, preferred_element_type=F32
            )
            skip = after - edge
            a_ref[after:size, edge:size] -= on_a[skip:, :]
            b_ref[after:size, 0:high] -= on_b[skip:, :]
    basis = lax.dot_general(
        second[...],
        b_ref[...],
        (((1,), (1,)), ((), ())),
        precision=HIGHEST,
        preferred_element_type=F32,
    )
    basis_ref[...] = (basis * scale_root).astype(BF16)


def factor_and_basis(mine, other, second, scale_root):
    rows, size = second.shape
    return pl.pallas_call(
        functools.partial(factor_kernel, scale_root),
        out_shape=(
            jax.ShapeDtypeStruct((rows, size), BF16),
            jax.ShapeDtypeStruct((size, size), F32),
        ),
        in_specs=[VMEM] * 3,
        out_specs=(VMEM, VMEM),
        scratch_shapes=[
            pltpu.VMEM((size, size), F32),
            pltpu.VMEM((size, size), F32),
            pltpu.VMEM((size + 16, size // 2), F32),
        ],
        name="factor_kernel",
        compiler_params=pltpu.CompilerParams(vmem_limit_bytes=16 << 20),
    )(mine, other, second)


def halo_step(send, swapped):
    slabs, bands = lax.axis_size("rows"), lax.axis_size("band")
    pairs = []
    for r in range(slabs):
        for b in range(bands):
            source = r - 1 if b < bands // 2 else r + 1
            if 0 <= source < slabs:
                pairs.append((source * bands + (b ^ 2 if swapped else b), r * bands + b))
    return lax.ppermute(send, ("rows", "band"), pairs)


def inner_step(halo):
    return flip(halo, "band", 1)


def add16(*parts):
    total = parts[0].astype(F32)
    for part in parts[1:]:
        total = total + part.astype(F32)
    return total.astype(BF16)


def per_device(coupling, sketch):
    slabs = lax.axis_size("rows")
    scale_root = math.sqrt(sketch.shape[0] * slabs)

    keep, send, edge, coupling, sketch = product(first_kernel, coupling, sketch)
    near = flip(send, "band", 1)
    halo = halo_step(edge, False)
    far = flip(add16(keep, near), "band", 2)
    halo2 = inner_step(halo)
    keep, send = product(late_kernel_slab, coupling, sketch, halo, halo2)
    own = add16(keep, flip(send, "band", 1), far)

    across = flip(own, "band", 2)
    halo = halo_step(across, False)
    own2 = flip(own, "band", 1)
    across2 = flip(across, "band", 1)
    keep, send = product(early_kernel, coupling, own, own2, across, across2)
    near = flip(send, "band", 1)
    far = flip(add16(keep, near), "band", 2)
    halo2 = inner_step(halo)
    keep, send = product(late_kernel, coupling, own, own2, halo, halo2)
    near = flip(send, "band", 1)

    second, mine, other = gram(keep, near, far)
    mine = mine + flip(other, "band", 1)
    mine = mine + flip(mine, "band", 2)
    bit = 1
    while bit < slabs:
        mine = mine + flip(mine, "rows", bit)
        bit *= 2
    other = flip(mine, "band", 1)
    return factor_and_basis(mine, other, second, scale_root)


def solution(mesh):
    in_specs = (P("rows", "band"), P("rows", None))
    out_specs = (P(("rows", "band"), None), P())

    return jax.shard_map(
        per_device, mesh=mesh, in_specs=in_specs, out_specs=out_specs, check_vma=False
    )
```

```python
import functools
import math

import jax
import jax.numpy as jnp
from jax import lax
from jax.experimental import pallas as pl
from jax.experimental.pallas import tpu as pltpu
from jax.sharding import PartitionSpec as P


HB = 1024
TB = 512
HIGHEST = lax.Precision.HIGHEST
F32 = jnp.float32
BF16 = jnp.bfloat16
NB = 64
PIV = 8
VMEM = pl.BlockSpec(memory_space=pltpu.VMEM)
IN_HBM = pl.BlockSpec(memory_space=pltpu.HBM)


def flip(array, axis, bit):
    count = lax.axis_size(axis)
    return lax.ppermute(array, axis, [(i, i ^ bit) for i in range(count)])


def place():
    band = lax.axis_index("band")
    return band, band // 2, band % 2


def tile_rows(base, tile):
    return pl.ds(pl.multiple_of(base + tile * TB, TB), TB)


def run_tiles(base, coupling, field, keep_ref, send_ref):
    band, half, core = place()
    width = coupling.shape[1]
    for tile, out in ((1 - core, send_ref), (core, keep_ref)):
        first = pl.multiple_of(tile * TB + band * width - half * HB, 128)
        out[...] = jnp.dot(
            coupling[tile_rows(base, tile), :],
            field[pl.ds(first, width), :],
            preferred_element_type=F32,
        ).astype(BF16)


def first_kernel(coupling, slab, keep_ref, send_ref, edge_ref, coupling_ref, slab_ref, sems):
    _, half, core = place()
    base = pl.multiple_of((1 - half) * HB, HB)
    late = pl.multiple_of(half * HB, HB)
    loads = [pltpu.make_async_copy(slab, slab_ref, sems.at[0])]
    for slot, start in ((1, base), (2, late)):
        rows = pl.ds(start, HB)
        loads.append(
            pltpu.make_async_copy(coupling.at[rows, :], coupling_ref.at[rows, :], sems.at[slot])
        )
    for load in loads:
        load.start()
    loads[0].wait()
    edge_ref[...] = slab_ref[tile_rows(base, core), :]
    loads[1].wait()
    run_tiles(base, coupling_ref, slab_ref, keep_ref, send_ref)
    loads[2].wait()


def early_kernel(coupling, own, own2, far, far2, keep_ref, send_ref, field):
    _, half, core = place()
    for ref, tile in (
        (own, 2 * half + core),
        (own2, 2 * half + 1 - core),
        (far, 2 * (1 - half) + core),
        (far2, 2 * (1 - half) + 1 - core),
    ):
        field[tile_rows(0, tile), :] = ref[...]
    run_tiles((1 - half) * HB, coupling, field, keep_ref, send_ref)


def late_kernel(coupling, near0, near1, halo, halo2, keep_ref, send_ref, field):
    _, half, core = place()
    near_at, halo_at = (1 - half) * HB, half * HB
    for ref, start, tile in (
        (near0, near_at, core),
        (near1, near_at, 1 - core),
        (halo, halo_at, core),
        (halo2, halo_at, 1 - core),
    ):
        field[tile_rows(start, tile), :] = ref[...]
    run_tiles(half * HB, coupling, field, keep_ref, send_ref)


def late_kernel_slab(coupling, slab, halo, halo2, keep_ref, send_ref, field):
    _, half, core = place()
    near_at, halo_at = pl.multiple_of((1 - half) * HB, HB), half * HB
    field[pl.ds(near_at, HB), :] = slab[pl.ds(pl.multiple_of(half * HB, HB), HB), :]
    for ref, tile in ((halo, core), (halo2, 1 - core)):
        field[tile_rows(halo_at, tile), :] = ref[...]
    run_tiles(half * HB, coupling, field, keep_ref, send_ref)


def product(kernel, coupling, *fields):
    width, columns = coupling.shape[1], fields[0].shape[1]
    first = kernel is first_kernel
    outputs = [jax.ShapeDtypeStruct((TB, columns), BF16)] * 2
    scratch = [pltpu.VMEM((2 * HB, columns), BF16)]
    if first:
        outputs += [outputs[0]] + [
            jax.ShapeDtypeStruct(array.shape, BF16) for array in (coupling, fields[0])
        ]
        scratch = [pltpu.SemaphoreType.DMA((3,))]
    operands = (coupling, *fields)
    if first:
        operands = [pltpu.with_memory_space_constraint(array, pltpu.HBM) for array in operands]
    return pl.pallas_call(
        kernel,
        out_shape=outputs,
        in_specs=[IN_HBM] * 2 if first else [VMEM] * (1 + len(fields)),
        out_specs=[VMEM] * len(outputs),
        scratch_shapes=scratch,
        compiler_params=pltpu.CompilerParams(vmem_limit_bytes=8 << 20),
        cost_estimate=pl.CostEstimate(
            flops=4 * TB * width * columns, bytes_accessed=4 * TB * width, transcendentals=0
        ),
    )(*operands)


def gram_kernel(keep, near, far, second_ref, mine_ref, other_ref, packed):
    core = lax.axis_index("band") % 2
    second = keep[...].astype(F32) + near[...].astype(F32) + far[...].astype(F32)
    second_ref[...] = second
    size = second.shape[1]
    mid = size // 2
    over_rows = (((0,), (0,)), ((), ()))
    top = lax.dot_general(
        second[:, :mid], second, over_rows, precision=HIGHEST, preferred_element_type=F32
    )
    low = lax.dot_general(
        second[:, mid:], second[:, mid:], over_rows, precision=HIGHEST, preferred_element_type=F32
    )
    row = lax.broadcasted_iota(jnp.int32, (mid, mid), 0)
    column = lax.broadcasted_iota(jnp.int32, (mid, mid), 1)
    packed[0:mid, :] = top[:, mid:]
    packed[mid:size, :] = jnp.where(column >= row, top[:, :mid], low)
    diagonal = jnp.sum(jnp.where(column == row, low, 0.0), axis=0, keepdims=True)
    packed[size:, :] = jnp.broadcast_to(diagonal, (16, mid))
    part = mid + 8
    mine_ref[...] = packed[pl.ds(pl.multiple_of(core * part, 8), part), :]
    other_ref[...] = packed[pl.ds(pl.multiple_of((1 - core) * part, 8), part), :]


def gram(keep, near, far):
    rows, size = keep.shape
    part = jax.ShapeDtypeStruct((size // 2 + 8, size // 2), F32)
    return pl.pallas_call(
        gram_kernel,
        out_shape=(jax.ShapeDtypeStruct((rows, size), F32), part, part),
        in_specs=[VMEM] * 3,
        out_specs=(VMEM,) * 3,
        scratch_shapes=[pltpu.VMEM((size + 16, size // 2), F32)],
        name="gram_kernel",
        compiler_params=pltpu.CompilerParams(vmem_limit_bytes=12 << 20),
    )(keep, near, far)


def factor_block(block):
    size = block.shape[0]
    groups = size // 8
    rows = [block[8 * i : 8 * i + 8, :] for i in range(groups)]
    shape = rows[0].shape
    sub = lax.broadcasted_iota(jnp.int32, shape, 0)
    for first in range(0, size, PIV):
        own, at = first // 8, first % 8
        pivots = range(PIV)
        row = [jnp.broadcast_to(rows[own][at + p : at + p + 1, :], shape) for p in pivots]
        column = [
            {
                q: jnp.broadcast_to(rows[q][:, first + p : first + p + 1], shape)
                for q in range(own, groups)
            }
            for p in pivots
        ]
        entry = {
            (p, t): jnp.broadcast_to(column[p][own][at + t : at + t + 1, :], shape)
            for p in pivots
            for t in range(p, PIV)
        }
        upper, scale = {}, []
        for p in pivots:
            if p % 2 == 0:
                q = p + 1
                root = lax.rsqrt(entry[p, p])
                minor = entry[p, p] * entry[q, q] - entry[p, q] * entry[p, q]
                scale += [root, lax.rsqrt(minor) * (entry[p, p] * root)]
            for t in range(p + 1, PIV):
                upper[p, t] = entry[p, t] * scale[p]
            for t in range(p + 1, PIV):
                for w in range(t, PIV):
                    entry[t, w] = entry[t, w] - upper[p, t] * upper[p, w]

        def solve(values):
            values = list(values)
            for p in pivots:
                values[p] = values[p] * scale[p]
                for t in range(p + 1, PIV):
                    values[t] = values[t] - upper[p, t] * values[p]
            return values

        done = solve(row)
        for q in range(own, groups):
            new = rows[q]
            if PIV < 8 or q > own:
                weight = solve([column[p][q] for p in pivots])
                total = weight[0] * done[0]
                for p in range(1, PIV):
                    total = total + weight[p] * done[p]
                new = new - total
            if q == own:
                new = jnp.where(sub >= at + PIV, new, rows[q])
                for p in pivots:
                    new = jnp.where(sub == at + p, done[p], new)
            rows[q] = new
    return jnp.concatenate(rows, 0)


def factor_kernel(scale_root, mine, other, second, basis_ref, factor_ref, packed):
    core = lax.axis_index("band") % 2
    part, mid = mine.shape
    size = 2 * mid
    packed[pl.ds(pl.multiple_of(core * part, 8), part), :] = mine[...]
    packed[pl.ds(pl.multiple_of((1 - core) * part, 8), part), :] = other[...]
    folded = packed[mid:size, :]
    turned = folded.T
    row = lax.broadcasted_iota(jnp.int32, (mid, mid), 0)
    column = lax.broadcasted_iota(jnp.int32, (mid, mid), 1)
    eye = row == column
    below = jnp.broadcast_to(packed[size : size + 1, :], (mid, mid))
    top = jnp.where(column >= row, folded, turned)
    low = jnp.where(column < row, folded, jnp.where(column > row, turned, below))

    diagonal = jnp.concatenate(
        [jnp.sum(jnp.where(eye, top, 0.0), axis=0, keepdims=True), packed[size : size + 1, :]], 1
    )
    root = lax.rsqrt(diagonal)

    def as_column(values):
        spread = jnp.where(eye, jnp.broadcast_to(values, (mid, mid)), 0.0)
        return jnp.sum(spread, axis=1, keepdims=True)

    top = jnp.concatenate([top, packed[0:mid, :]], 1) * root * as_column(root[:, :mid])
    low = low * root[:, mid:] * as_column(root[:, mid:])
    scaled = second[...] * (root * scale_root)
    length = diagonal * root * (1.0 / scale_root)

    lane = lax.broadcasted_iota(jnp.int32, (NB, 128), 1)
    line = lax.broadcasted_iota(jnp.int32, (NB, 128), 0)
    over_rows = (((0,), (0,)), ((), ()))

    def times(a, b, dims=(((1,), (0,)), ((), ()))):
        return lax.dot_general(a, b, dims, precision=HIGHEST, preferred_element_type=F32)

    def widen(value, width, before=0):
        parts = [value]
        if before:
            parts.insert(0, jnp.zeros((NB, before), F32))
        after = width - before - value.shape[1]
        if after:
            parts.append(jnp.zeros((NB, after), F32))
        return jnp.concatenate(parts, 1) if len(parts) > 1 else value

    count = size // NB
    start = [k * NB // 128 * 128 for k in range(count)]
    ahead = [
        top[k * NB : (k + 1) * NB, :] if start[k] == 0 else low[k * NB - mid : (k + 1) * NB - mid, :]
        for k in range(count)
    ]
    behind = [None] * count
    inverse = []
    for k in range(count):
        shift = k * NB - start[k]
        block = ahead[k][:, :128]
        if shift:
            block = pltpu.roll(block, 128 - shift, 1)
        block = factor_block(jnp.where(lane < NB, block, jnp.where(lane - NB == line, 1.0, 0.0)))
        upper = jnp.where((lane < NB) & (lane >= line), block, 0.0)
        lower = jnp.where(lane <= line, pltpu.roll(block, 128 - NB, 1), 0.0)[:, :NB]
        if shift:
            upper = pltpu.roll(upper, shift, 1)
        width = size - start[k]
        upper = widen(upper, width)
        if k + 1 < count:
            right = times(lower, ahead[k])
            place_of = lax.broadcasted_iota(jnp.int32, (NB, width), 1) + start[k]
            right = jnp.where(place_of >= (k + 1) * NB, right, 0.0)
            upper = upper + right
            for i in range(k + 1, count):
                at = i * NB - start[k]
                ahead[i] = ahead[i] - times(
                    right[:, at : at + NB], right[:, start[i] - start[k] :], over_rows
                )
        rows = slice(k * NB, (k + 1) * NB)
        if start[k]:
            factor_ref[rows, 0 : start[k]] = jnp.zeros((NB, start[k]), F32)
        factor_ref[rows, start[k] :] = upper * length[:, start[k] :]
        reach = start[k] + 128
        own = widen(lower, 128)
        if shift:
            own = pltpu.roll(own, shift, 1)
        left = widen(own, reach, start[k])
        if behind[k] is not None:
            left = left + times(lower, widen(behind[k], reach))
        inverse.append(widen(left, size))
        for i in range(k + 1, count):
            at = i * NB - start[k]
            change = times(right[:, at : at + NB], left, over_rows)
            behind[i] = -change if behind[i] is None else widen(behind[i], reach) - change
    basis = times(scaled, jnp.concatenate(inverse, 0), (((1,), (1,)), ((), ())))
    basis_ref[...] = basis.astype(BF16)


def factor_and_basis(mine, other, second, scale_root):
    rows, size = second.shape
    return pl.pallas_call(
        functools.partial(factor_kernel, scale_root),
        out_shape=(
            jax.ShapeDtypeStruct((rows, size), BF16),
            jax.ShapeDtypeStruct((size, size), F32),
        ),
        in_specs=[VMEM] * 3,
        out_specs=(VMEM, VMEM),
        scratch_shapes=[
            pltpu.VMEM((size + 16, size // 2), F32),
        ],
        name="factor_kernel",
        compiler_params=pltpu.CompilerParams(vmem_limit_bytes=16 << 20),
    )(mine, other, second)


def halo_step(send, swapped):
    slabs, bands = lax.axis_size("rows"), lax.axis_size("band")
    pairs = []
    for r in range(slabs):
        for b in range(bands):
            source = r - 1 if b < bands // 2 else r + 1
            if 0 <= source < slabs:
                pairs.append((source * bands + (b ^ 2 if swapped else b), r * bands + b))
    return lax.ppermute(send, ("rows", "band"), pairs)


def inner_step(halo):
    return flip(halo, "band", 1)


def doubling_steps(slabs, bands):
    levels = [2] + [bit * bands for bit in (1 << i for i in range(slabs.bit_length() - 1))]
    turn = len(levels) // 2
    orders = (levels, levels[turn:] + levels[:turn])
    return [
        [(d, d ^ orders[d % 2][step]) for d in range(slabs * bands)] for step in range(len(levels))
    ]


def add16(*parts):
    total = parts[0].astype(F32)
    for part in parts[1:]:
        total = total + part.astype(F32)
    return total.astype(BF16)


def per_device(coupling, sketch):
    slabs = lax.axis_size("rows")
    scale_root = math.sqrt(sketch.shape[0] * slabs)

    keep, send, edge, coupling, sketch = product(first_kernel, coupling, sketch)
    near = flip(send, "band", 1)
    halo = halo_step(edge, False)
    far = flip(add16(keep, near), "band", 2)
    halo2 = inner_step(halo)
    keep, send = product(late_kernel_slab, coupling, sketch, halo, halo2)
    own = add16(keep, flip(send, "band", 1), far)

    across = flip(own, "band", 2)
    halo = halo_step(across, False)
    own2 = flip(own, "band", 1)
    across2 = flip(across, "band", 1)
    keep, send = product(early_kernel, coupling, own, own2, across, across2)
    near = flip(send, "band", 1)
    far = flip(add16(keep, near), "band", 2)
    halo2 = inner_step(halo)
    keep, send = product(late_kernel, coupling, own, own2, halo, halo2)
    near = flip(send, "band", 1)

    second, mine, other = gram(keep, near, far)
    mine = mine + flip(other, "band", 1)
    for pairs in doubling_steps(slabs, lax.axis_size("band")):
        mine = mine + lax.ppermute(mine, ("rows", "band"), pairs)
    other = flip(mine, "band", 1)
    return factor_and_basis(mine, other, second, scale_root)


def solution(mesh):
    in_specs = (P("rows", "band"), P("rows", None))
    out_specs = (P(("rows", "band"), None), P())

    return jax.shard_map(
        per_device, mesh=mesh, in_specs=in_specs, out_specs=out_specs, check_vma=False
    )
```

```python
import functools
import math

import jax
import jax.numpy as jnp
from jax import lax
from jax.experimental import pallas as pl
from jax.experimental.pallas import tpu as pltpu
from jax.sharding import PartitionSpec as P


HB = 1024
TB = 512
HIGHEST = lax.Precision.HIGHEST
F32 = jnp.float32
BF16 = jnp.bfloat16
NB = 64
PIV = 8
VMEM = pl.BlockSpec(memory_space=pltpu.VMEM)
IN_HBM = pl.BlockSpec(memory_space=pltpu.HBM)


def flip(array, axis, bit):
    count = lax.axis_size(axis)
    return lax.ppermute(array, axis, [(i, i ^ bit) for i in range(count)])


def place():
    band = lax.axis_index("band")
    return band, band // 2, band % 2


def tile_rows(base, tile):
    return pl.ds(pl.multiple_of(base + tile * TB, TB), TB)


def run_tiles(base, coupling, field, keep_ref, send_ref):
    band, half, core = place()
    width = coupling.shape[1]
    for tile, out in ((1 - core, send_ref), (core, keep_ref)):
        first = pl.multiple_of(tile * TB + band * width - half * HB, 128)
        out[...] = jnp.dot(
            coupling[tile_rows(base, tile), :],
            field[pl.ds(first, width), :],
            preferred_element_type=F32,
        ).astype(BF16)


def first_kernel(coupling, slab, keep_ref, send_ref, coupling_ref, slab_ref, sems):
    _, half, _ = place()
    base = pl.multiple_of((1 - half) * HB, HB)
    late = pl.multiple_of(half * HB, HB)
    loads = [pltpu.make_async_copy(slab, slab_ref, sems.at[0])]
    for slot, start in ((1, base), (2, late)):
        rows = pl.ds(start, HB)
        loads.append(
            pltpu.make_async_copy(coupling.at[rows, :], coupling_ref.at[rows, :], sems.at[slot])
        )
    for load in loads:
        load.start()
    loads[0].wait()
    loads[1].wait()
    run_tiles(base, coupling_ref, slab_ref, keep_ref, send_ref)
    loads[2].wait()


def early_kernel(coupling, own, own2, far, far2, keep_ref, send_ref, field):
    _, half, core = place()
    for ref, tile in (
        (own, 2 * half + core),
        (own2, 2 * half + 1 - core),
        (far, 2 * (1 - half) + core),
        (far2, 2 * (1 - half) + 1 - core),
    ):
        field[tile_rows(0, tile), :] = ref[...]
    run_tiles((1 - half) * HB, coupling, field, keep_ref, send_ref)


def late_kernel(coupling, near0, near1, halo, halo2, keep_ref, send_ref, field):
    _, half, core = place()
    near_at, halo_at = (1 - half) * HB, half * HB
    for ref, start, tile in (
        (near0, near_at, core),
        (near1, near_at, 1 - core),
        (halo, halo_at, core),
        (halo2, halo_at, 1 - core),
    ):
        field[tile_rows(start, tile), :] = ref[...]
    run_tiles(half * HB, coupling, field, keep_ref, send_ref)


def late_kernel_slab(coupling, slab, halo, halo2, keep_ref, send_ref, field):
    _, half, core = place()
    near_at, halo_at = pl.multiple_of((1 - half) * HB, HB), half * HB
    field[pl.ds(near_at, HB), :] = slab[pl.ds(pl.multiple_of(half * HB, HB), HB), :]
    for ref, tile in ((halo, core), (halo2, 1 - core)):
        field[tile_rows(halo_at, tile), :] = ref[...]
    run_tiles(half * HB, coupling, field, keep_ref, send_ref)


def product(kernel, coupling, *fields):
    width, columns = coupling.shape[1], fields[0].shape[1]
    first = kernel is first_kernel
    outputs = [jax.ShapeDtypeStruct((TB, columns), BF16)] * 2
    scratch = [pltpu.VMEM((2 * HB, columns), BF16)]
    if first:
        outputs += [
            jax.ShapeDtypeStruct(array.shape, BF16) for array in (coupling, fields[0])
        ]
        scratch = [pltpu.SemaphoreType.DMA((3,))]
    operands = (coupling, *fields)
    if first:
        operands = [pltpu.with_memory_space_constraint(array, pltpu.HBM) for array in operands]
    return pl.pallas_call(
        kernel,
        out_shape=outputs,
        in_specs=[IN_HBM] * 2 if first else [VMEM] * (1 + len(fields)),
        out_specs=[VMEM] * len(outputs),
        scratch_shapes=scratch,
        compiler_params=pltpu.CompilerParams(vmem_limit_bytes=8 << 20),
        cost_estimate=pl.CostEstimate(
            flops=4 * TB * width * columns, bytes_accessed=4 * TB * width, transcendentals=0
        ),
    )(*operands)


def gram_kernel(keep, near, far, second_ref, mine_ref, other_ref, packed):
    core = lax.axis_index("band") % 2
    second = keep[...].astype(F32) + near[...].astype(F32) + far[...].astype(F32)
    second_ref[...] = second
    size = second.shape[1]
    mid = size // 2
    over_rows = (((0,), (0,)), ((), ()))
    top = lax.dot_general(
        second[:, :mid], second, over_rows, precision=HIGHEST, preferred_element_type=F32
    )
    low = lax.dot_general(
        second[:, mid:], second[:, mid:], over_rows, precision=HIGHEST, preferred_element_type=F32
    )
    row = lax.broadcasted_iota(jnp.int32, (mid, mid), 0)
    column = lax.broadcasted_iota(jnp.int32, (mid, mid), 1)
    packed[0:mid, :] = top[:, mid:]
    packed[mid:size, :] = jnp.where(column >= row, top[:, :mid], low)
    diagonal = jnp.sum(jnp.where(column == row, low, 0.0), axis=0, keepdims=True)
    packed[size:, :] = jnp.broadcast_to(diagonal, (16, mid))
    part = mid + 8
    mine_ref[...] = packed[pl.ds(pl.multiple_of(core * part, 8), part), :]
    other_ref[...] = packed[pl.ds(pl.multiple_of((1 - core) * part, 8), part), :]


def gram(keep, near, far):
    rows, size = keep.shape
    part = jax.ShapeDtypeStruct((size // 2 + 8, size // 2), F32)
    return pl.pallas_call(
        gram_kernel,
        out_shape=(jax.ShapeDtypeStruct((rows, size), F32), part, part),
        in_specs=[VMEM] * 3,
        out_specs=(VMEM,) * 3,
        scratch_shapes=[pltpu.VMEM((size + 16, size // 2), F32)],
        name="gram_kernel",
        compiler_params=pltpu.CompilerParams(vmem_limit_bytes=12 << 20),
    )(keep, near, far)


def factor_block(block):
    size = block.shape[0]
    groups = size // 8
    rows = [block[8 * i : 8 * i + 8, :] for i in range(groups)]
    shape = rows[0].shape
    sub = lax.broadcasted_iota(jnp.int32, shape, 0)
    for first in range(0, size, PIV):
        own, at = first // 8, first % 8
        pivots = range(PIV)
        row = [jnp.broadcast_to(rows[own][at + p : at + p + 1, :], shape) for p in pivots]
        column = [
            {
                q: jnp.broadcast_to(rows[q][:, first + p : first + p + 1], shape)
                for q in range(own, groups)
            }
            for p in pivots
        ]
        entry = {
            (p, t): jnp.take_along_axis(
                column[p][own], jnp.full(shape, at + t, jnp.int32), axis=0
            )
            for p in pivots
            for t in range(p, PIV)
        }
        upper, scale = {}, []
        for p in pivots:
            if p % 2 == 0:
                q = p + 1
                root = lax.rsqrt(entry[p, p])
                minor = entry[p, p] * entry[q, q] - entry[p, q] * entry[p, q]
                scale += [root, lax.rsqrt(minor) * (entry[p, p] * root)]
            for t in range(p + 1, PIV):
                upper[p, t] = entry[p, t] * scale[p]
            for t in range(p + 1, PIV):
                for w in range(t, PIV):
                    entry[t, w] = entry[t, w] - upper[p, t] * upper[p, w]

        def solve(values):
            values = list(values)
            for p in pivots:
                values[p] = values[p] * scale[p]
                for t in range(p + 1, PIV):
                    values[t] = values[t] - upper[p, t] * values[p]
            return values

        done = solve(row)
        for q in range(own, groups):
            new = rows[q]
            if PIV < 8 or q > own:
                weight = solve([column[p][q] for p in pivots])
                total = weight[0] * done[0]
                for p in range(1, PIV):
                    total = total + weight[p] * done[p]
                new = new - total
            if q == own:
                new = jnp.where(sub >= at + PIV, new, rows[q])
                for p in pivots:
                    new = jnp.where(sub == at + p, done[p], new)
            rows[q] = new
    return jnp.concatenate(rows, 0)


def factor_kernel(scale_root, mine, other, second, basis_ref, factor_ref, packed):
    core = lax.axis_index("band") % 2
    part, mid = mine.shape
    size = 2 * mid
    packed[pl.ds(pl.multiple_of(core * part, 8), part), :] = mine[...]
    packed[pl.ds(pl.multiple_of((1 - core) * part, 8), part), :] = other[...]
    folded = packed[mid:size, :]
    turned = folded.T
    row = lax.broadcasted_iota(jnp.int32, (mid, mid), 0)
    column = lax.broadcasted_iota(jnp.int32, (mid, mid), 1)
    eye = row == column
    below = jnp.broadcast_to(packed[size : size + 1, :], (mid, mid))
    top = jnp.where(column >= row, folded, turned)
    low = jnp.where(column < row, folded, jnp.where(column > row, turned, below))

    diagonal = jnp.concatenate(
        [jnp.sum(jnp.where(eye, top, 0.0), axis=0, keepdims=True), packed[size : size + 1, :]], 1
    )
    root = lax.rsqrt(diagonal)

    def as_column(values):
        spread = jnp.where(eye, jnp.broadcast_to(values, (mid, mid)), 0.0)
        return jnp.sum(spread, axis=1, keepdims=True)

    top = jnp.concatenate([top, packed[0:mid, :]], 1) * root * as_column(root[:, :mid])
    low = low * root[:, mid:] * as_column(root[:, mid:])
    scaled = second[...] * (root * scale_root)
    length = diagonal * root * (1.0 / scale_root)

    lane = lax.broadcasted_iota(jnp.int32, (NB, 128), 1)
    line = lax.broadcasted_iota(jnp.int32, (NB, 128), 0)
    over_rows = (((0,), (0,)), ((), ()))

    def times(a, b, dims=(((1,), (0,)), ((), ()))):
        return lax.dot_general(a, b, dims, precision=HIGHEST, preferred_element_type=F32)

    def widen(value, width, before=0):
        parts = [value]
        if before:
            parts.insert(0, jnp.zeros((NB, before), F32))
        after = width - before - value.shape[1]
        if after:
            parts.append(jnp.zeros((NB, after), F32))
        return jnp.concatenate(parts, 1) if len(parts) > 1 else value

    count = size // NB
    start = [k * NB // 128 * 128 for k in range(count)]
    ahead = [
        top[k * NB : (k + 1) * NB, :] if start[k] == 0 else low[k * NB - mid : (k + 1) * NB - mid, :]
        for k in range(count)
    ]
    behind = [None] * count
    inverse = []
    for k in range(count):
        shift = k * NB - start[k]
        block = ahead[k][:, :128]
        if shift:
            block = pltpu.roll(block, 128 - shift, 1)
        block = factor_block(jnp.where(lane < NB, block, jnp.where(lane - NB == line, 1.0, 0.0)))
        upper = jnp.where((lane < NB) & (lane >= line), block, 0.0)
        lower = jnp.where(lane <= line, pltpu.roll(block, 128 - NB, 1), 0.0)[:, :NB]
        if shift:
            upper = pltpu.roll(upper, shift, 1)
        width = size - start[k]
        upper = widen(upper, width)
        if k + 1 < count:
            right = times(lower, ahead[k])
            place_of = lax.broadcasted_iota(jnp.int32, (NB, width), 1) + start[k]
            right = jnp.where(place_of >= (k + 1) * NB, right, 0.0)
            upper = upper + right
            for i in range(k + 1, count):
                at = i * NB - start[k]
                ahead[i] = ahead[i] - times(
                    right[:, at : at + NB], right[:, start[i] - start[k] :], over_rows
                )
        rows = slice(k * NB, (k + 1) * NB)
        if start[k]:
            factor_ref[rows, 0 : start[k]] = jnp.zeros((NB, start[k]), F32)
        factor_ref[rows, start[k] :] = upper * length[:, start[k] :]
        reach = start[k] + 128
        own = widen(lower, 128)
        if shift:
            own = pltpu.roll(own, shift, 1)
        left = widen(own, reach, start[k])
        if behind[k] is not None:
            left = left + times(lower, widen(behind[k], reach))
        inverse.append(widen(left, size))
        for i in range(k + 1, count):
            at = i * NB - start[k]
            change = times(right[:, at : at + NB], left, over_rows)
            behind[i] = -change if behind[i] is None else widen(behind[i], reach) - change
    basis = times(scaled, jnp.concatenate(inverse, 0), (((1,), (1,)), ((), ())))
    basis_ref[...] = basis.astype(BF16)


def factor_and_basis(mine, other, second, scale_root):
    rows, size = second.shape
    return pl.pallas_call(
        functools.partial(factor_kernel, scale_root),
        out_shape=(
            jax.ShapeDtypeStruct((rows, size), BF16),
            jax.ShapeDtypeStruct((size, size), F32),
        ),
        in_specs=[VMEM] * 3,
        out_specs=(VMEM, VMEM),
        scratch_shapes=[
            pltpu.VMEM((size + 16, size // 2), F32),
        ],
        name="factor_kernel",
        compiler_params=pltpu.CompilerParams(vmem_limit_bytes=16 << 20),
    )(mine, other, second)


def halo_step(send, swapped):
    slabs, bands = lax.axis_size("rows"), lax.axis_size("band")
    pairs = []
    for r in range(slabs):
        for b in range(bands):
            source = r - 1 if b < bands // 2 else r + 1
            if 0 <= source < slabs:
                pairs.append((source * bands + (b ^ 2 if swapped else b), r * bands + b))
    return lax.ppermute(send, ("rows", "band"), pairs)


def inner_step(halo):
    return flip(halo, "band", 1)


def doubling_steps(slabs, bands):
    levels = [2] + [bit * bands for bit in (1 << i for i in range(slabs.bit_length() - 1))]
    turn = len(levels) // 2
    orders = (levels, levels[turn:] + levels[:turn])
    return [
        [(d, d ^ orders[d % 2][step]) for d in range(slabs * bands)] for step in range(len(levels))
    ]


def add16(*parts):
    total = parts[0].astype(F32)
    for part in parts[1:]:
        total = total + part.astype(F32)
    return total.astype(BF16)


def per_device(coupling, sketch):
    slabs = lax.axis_size("rows")
    scale_root = math.sqrt(sketch.shape[0] * slabs)

    band = lax.axis_index("band")
    edge_at = (1 - band // 2) * HB + band % 2 * TB
    halo = halo_step(lax.dynamic_slice_in_dim(sketch, edge_at, TB, 0), False)
    keep, send, coupling, sketch = product(first_kernel, coupling, sketch)
    near = flip(send, "band", 1)
    far = flip(add16(keep, near), "band", 2)
    halo2 = inner_step(halo)
    keep, send = product(late_kernel_slab, coupling, sketch, halo, halo2)
    own = add16(keep, flip(send, "band", 1), far)

    across = flip(own, "band", 2)
    halo = halo_step(across, False)
    own2 = flip(own, "band", 1)
    across2 = flip(across, "band", 1)
    keep, send = product(early_kernel, coupling, own, own2, across, across2)
    near = flip(send, "band", 1)
    far = flip(add16(keep, near), "band", 2)
    halo2 = inner_step(halo)
    keep, send = product(late_kernel, coupling, own, own2, halo, halo2)
    near = flip(send, "band", 1)

    second, mine, other = gram(keep, near, far)
    mine = mine + flip(other, "band", 1)
    for pairs in doubling_steps(slabs, lax.axis_size("band")):
        mine = mine + lax.ppermute(mine, ("rows", "band"), pairs)
    other = flip(mine, "band", 1)
    return factor_and_basis(mine, other, second, scale_root)


def solution(mesh):
    in_specs = (P("rows", "band"), P("rows", None))
    out_specs = (P(("rows", "band"), None), P())

    return jax.shard_map(
        per_device, mesh=mesh, in_specs=in_specs, out_specs=out_specs, check_vma=False
    )
```

```python
import functools
import math

import jax
import jax.numpy as jnp
from jax import lax
from jax.experimental import pallas as pl
from jax.experimental.pallas import tpu as pltpu
from jax.sharding import PartitionSpec as P


HB = 1024
TB = 512
HIGHEST = lax.Precision.HIGHEST
F32 = jnp.float32
BF16 = jnp.bfloat16
NB = 64
PIV = 8
VMEM = pl.BlockSpec(memory_space=pltpu.VMEM)
IN_HBM = pl.BlockSpec(memory_space=pltpu.HBM)


def flip(array, axis, bit):
    count = lax.axis_size(axis)
    return lax.ppermute(array, axis, [(i, i ^ bit) for i in range(count)])


def place():
    band = lax.axis_index("band")
    return band, band // 2, band % 2


def tile_rows(base, tile):
    return pl.ds(pl.multiple_of(base + tile * TB, TB), TB)


def run_tiles(base, coupling, field, keep_ref, send_ref):
    band, half, core = place()
    width = coupling.shape[1]
    for tile, out in ((1 - core, send_ref), (core, keep_ref)):
        first = pl.multiple_of(tile * TB + band * width - half * HB, 128)
        out[...] = jnp.dot(
            coupling[tile_rows(base, tile), :],
            field[pl.ds(first, width), :],
            preferred_element_type=F32,
        ).astype(BF16)


def edge_kernel(slab, edge_ref, sem):
    _, half, core = place()
    load = pltpu.make_async_copy(slab.at[tile_rows((1 - half) * HB, core), :], edge_ref, sem)
    load.start()
    load.wait()


def edge_of(slab):
    return pl.pallas_call(
        edge_kernel,
        out_shape=jax.ShapeDtypeStruct((TB, slab.shape[1]), BF16),
        in_specs=[IN_HBM],
        out_specs=VMEM,
        scratch_shapes=[pltpu.SemaphoreType.DMA],
        name="edge_kernel",
        compiler_params=pltpu.CompilerParams(vmem_limit_bytes=1 << 20),
    )(pltpu.with_memory_space_constraint(slab, pltpu.HBM))


def first_kernel(coupling, slab, keep_ref, send_ref, coupling_ref, slab_ref, sems):
    _, half, _ = place()
    base = pl.multiple_of((1 - half) * HB, HB)
    late = pl.multiple_of(half * HB, HB)
    loads = [pltpu.make_async_copy(slab, slab_ref, sems.at[0])]
    for slot, start in ((1, base), (2, late)):
        rows = pl.ds(start, HB)
        loads.append(
            pltpu.make_async_copy(coupling.at[rows, :], coupling_ref.at[rows, :], sems.at[slot])
        )
    for load in loads:
        load.start()
    loads[0].wait()
    loads[1].wait()
    run_tiles(base, coupling_ref, slab_ref, keep_ref, send_ref)
    loads[2].wait()


def early_kernel(coupling, own, own2, far, far2, keep_ref, send_ref, field):
    _, half, core = place()
    for ref, tile in (
        (own, 2 * half + core),
        (own2, 2 * half + 1 - core),
        (far, 2 * (1 - half) + core),
        (far2, 2 * (1 - half) + 1 - core),
    ):
        field[tile_rows(0, tile), :] = ref[...]
    run_tiles((1 - half) * HB, coupling, field, keep_ref, send_ref)


def late_kernel(coupling, near0, near1, halo, halo2, keep_ref, send_ref, field):
    _, half, core = place()
    near_at, halo_at = (1 - half) * HB, half * HB
    for ref, start, tile in (
        (near0, near_at, core),
        (near1, near_at, 1 - core),
        (halo, halo_at, core),
        (halo2, halo_at, 1 - core),
    ):
        field[tile_rows(start, tile), :] = ref[...]
    run_tiles(half * HB, coupling, field, keep_ref, send_ref)


def late_kernel_slab(coupling, slab, halo, halo2, keep_ref, send_ref, field):
    _, half, core = place()
    near_at, halo_at = pl.multiple_of((1 - half) * HB, HB), half * HB
    field[pl.ds(near_at, HB), :] = slab[pl.ds(pl.multiple_of(half * HB, HB), HB), :]
    for ref, tile in ((halo, core), (halo2, 1 - core)):
        field[tile_rows(halo_at, tile), :] = ref[...]
    run_tiles(half * HB, coupling, field, keep_ref, send_ref)


def product(kernel, coupling, *fields):
    width, columns = coupling.shape[1], fields[0].shape[1]
    first = kernel is first_kernel
    outputs = [jax.ShapeDtypeStruct((TB, columns), BF16)] * 2
    scratch = [pltpu.VMEM((2 * HB, columns), BF16)]
    if first:
        outputs += [
            jax.ShapeDtypeStruct(array.shape, BF16) for array in (coupling, fields[0])
        ]
        scratch = [pltpu.SemaphoreType.DMA((3,))]
    operands = (coupling, *fields)
    if first:
        operands = [pltpu.with_memory_space_constraint(array, pltpu.HBM) for array in operands]
    return pl.pallas_call(
        kernel,
        out_shape=outputs,
        in_specs=[IN_HBM] * 2 if first else [VMEM] * (1 + len(fields)),
        out_specs=[VMEM] * len(outputs),
        scratch_shapes=scratch,
        compiler_params=pltpu.CompilerParams(vmem_limit_bytes=8 << 20),
        cost_estimate=pl.CostEstimate(
            flops=4 * TB * width * columns, bytes_accessed=4 * TB * width, transcendentals=0
        ),
    )(*operands)


def gram_kernel(keep, near, far, second_ref, mine_ref, other_ref, packed):
    core = lax.axis_index("band") % 2
    second = keep[...].astype(F32) + near[...].astype(F32) + far[...].astype(F32)
    second_ref[...] = second
    size = second.shape[1]
    mid = size // 2
    over_rows = (((0,), (0,)), ((), ()))
    top = lax.dot_general(
        second[:, :mid], second, over_rows, precision=HIGHEST, preferred_element_type=F32
    )
    low = lax.dot_general(
        second[:, mid:], second[:, mid:], over_rows, precision=HIGHEST, preferred_element_type=F32
    )
    row = lax.broadcasted_iota(jnp.int32, (mid, mid), 0)
    column = lax.broadcasted_iota(jnp.int32, (mid, mid), 1)
    packed[0:mid, :] = top[:, mid:]
    packed[mid:size, :] = jnp.where(column >= row, top[:, :mid], low)
    diagonal = jnp.sum(jnp.where(column == row, low, 0.0), axis=0, keepdims=True)
    packed[size:, :] = jnp.broadcast_to(diagonal, (16, mid))
    part = mid + 8
    mine_ref[...] = packed[pl.ds(pl.multiple_of(core * part, 8), part), :]
    other_ref[...] = packed[pl.ds(pl.multiple_of((1 - core) * part, 8), part), :]


def gram(keep, near, far):
    rows, size = keep.shape
    part = jax.ShapeDtypeStruct((size // 2 + 8, size // 2), F32)
    return pl.pallas_call(
        gram_kernel,
        out_shape=(jax.ShapeDtypeStruct((rows, size), F32), part, part),
        in_specs=[VMEM] * 3,
        out_specs=(VMEM,) * 3,
        scratch_shapes=[pltpu.VMEM((size + 16, size // 2), F32)],
        name="gram_kernel",
        compiler_params=pltpu.CompilerParams(vmem_limit_bytes=12 << 20),
    )(keep, near, far)


def factor_block(block):
    size = block.shape[0]
    groups = size // 8
    rows = [block[8 * i : 8 * i + 8, :] for i in range(groups)]
    shape = rows[0].shape
    sub = lax.broadcasted_iota(jnp.int32, shape, 0)
    for first in range(0, size, PIV):
        own, at = first // 8, first % 8
        pivots = range(PIV)
        row = [jnp.broadcast_to(rows[own][at + p : at + p + 1, :], shape) for p in pivots]
        column = [
            {
                q: jnp.broadcast_to(rows[q][:, first + p : first + p + 1], shape)
                for q in range(own, groups)
            }
            for p in pivots
        ]
        entry = {
            (p, t): jnp.take_along_axis(
                column[p][own], jnp.full(shape, at + t, jnp.int32), axis=0
            )
            for p in pivots
            for t in range(p, PIV)
        }
        upper, scale = {}, []
        for p in pivots:
            if p % 2 == 0:
                q = p + 1
                root = lax.rsqrt(entry[p, p])
                minor = entry[p, p] * entry[q, q] - entry[p, q] * entry[p, q]
                scale += [root, lax.rsqrt(minor) * (entry[p, p] * root)]
            for t in range(p + 1, PIV):
                upper[p, t] = entry[p, t] * scale[p]
            for t in range(p + 1, PIV):
                for w in range(t, PIV):
                    entry[t, w] = entry[t, w] - upper[p, t] * upper[p, w]

        def solve(values):
            values = list(values)
            for p in pivots:
                values[p] = values[p] * scale[p]
                for t in range(p + 1, PIV):
                    values[t] = values[t] - upper[p, t] * values[p]
            return values

        done = solve(row)
        for q in range(own, groups):
            new = rows[q]
            if PIV < 8 or q > own:
                weight = solve([column[p][q] for p in pivots])
                total = weight[0] * done[0]
                for p in range(1, PIV):
                    total = total + weight[p] * done[p]
                new = new - total
            if q == own:
                new = jnp.where(sub >= at + PIV, new, rows[q])
                for p in pivots:
                    new = jnp.where(sub == at + p, done[p], new)
            rows[q] = new
    return jnp.concatenate(rows, 0)


def factor_kernel(scale_root, mine, other, second, basis_ref, factor_ref, packed):
    core = lax.axis_index("band") % 2
    part, mid = mine.shape
    size = 2 * mid
    packed[pl.ds(pl.multiple_of(core * part, 8), part), :] = mine[...]
    packed[pl.ds(pl.multiple_of((1 - core) * part, 8), part), :] = other[...]
    folded = packed[mid:size, :]
    turned = folded.T
    row = lax.broadcasted_iota(jnp.int32, (mid, mid), 0)
    column = lax.broadcasted_iota(jnp.int32, (mid, mid), 1)
    eye = row == column
    below = jnp.broadcast_to(packed[size : size + 1, :], (mid, mid))
    top = jnp.where(column >= row, folded, turned)
    low = jnp.where(column < row, folded, jnp.where(column > row, turned, below))

    diagonal = jnp.concatenate(
        [jnp.sum(jnp.where(eye, top, 0.0), axis=0, keepdims=True), packed[size : size + 1, :]], 1
    )
    root = lax.rsqrt(diagonal)

    def as_column(values):
        spread = jnp.where(eye, jnp.broadcast_to(values, (mid, mid)), 0.0)
        return jnp.sum(spread, axis=1, keepdims=True)

    top = jnp.concatenate([top, packed[0:mid, :]], 1) * root * as_column(root[:, :mid])
    low = low * root[:, mid:] * as_column(root[:, mid:])
    scaled = second[...] * (root * scale_root)
    length = diagonal * root * (1.0 / scale_root)

    lane = lax.broadcasted_iota(jnp.int32, (NB, 128), 1)
    line = lax.broadcasted_iota(jnp.int32, (NB, 128), 0)
    over_rows = (((0,), (0,)), ((), ()))

    def times(a, b, dims=(((1,), (0,)), ((), ()))):
        return lax.dot_general(a, b, dims, precision=HIGHEST, preferred_element_type=F32)

    def widen(value, width, before=0):
        parts = [value]
        if before:
            parts.insert(0, jnp.zeros((NB, before), F32))
        after = width - before - value.shape[1]
        if after:
            parts.append(jnp.zeros((NB, after), F32))
        return jnp.concatenate(parts, 1) if len(parts) > 1 else value

    count = size // NB
    start = [k * NB // 128 * 128 for k in range(count)]
    ahead = [
        top[k * NB : (k + 1) * NB, :] if start[k] == 0 else low[k * NB - mid : (k + 1) * NB - mid, :]
        for k in range(count)
    ]
    behind = [None] * count
    inverse = []
    for k in range(count):
        shift = k * NB - start[k]
        block = ahead[k][:, :128]
        if shift:
            block = pltpu.roll(block, 128 - shift, 1)
        block = factor_block(jnp.where(lane < NB, block, jnp.where(lane - NB == line, 1.0, 0.0)))
        upper = jnp.where((lane < NB) & (lane >= line), block, 0.0)
        lower = jnp.where(lane <= line, pltpu.roll(block, 128 - NB, 1), 0.0)[:, :NB]
        if shift:
            upper = pltpu.roll(upper, shift, 1)
        width = size - start[k]
        upper = widen(upper, width)
        if k + 1 < count:
            right = times(lower, ahead[k])
            place_of = lax.broadcasted_iota(jnp.int32, (NB, width), 1) + start[k]
            right = jnp.where(place_of >= (k + 1) * NB, right, 0.0)
            upper = upper + right
            for i in range(k + 1, count):
                at = i * NB - start[k]
                ahead[i] = ahead[i] - times(
                    right[:, at : at + NB], right[:, start[i] - start[k] :], over_rows
                )
        rows = slice(k * NB, (k + 1) * NB)
        if start[k]:
            factor_ref[rows, 0 : start[k]] = jnp.zeros((NB, start[k]), F32)
        factor_ref[rows, start[k] :] = upper * length[:, start[k] :]
        reach = start[k] + 128
        own = widen(lower, 128)
        if shift:
            own = pltpu.roll(own, shift, 1)
        left = widen(own, reach, start[k])
        if behind[k] is not None:
            left = left + times(lower, widen(behind[k], reach))
        inverse.append(widen(left, size))
        for i in range(k + 1, count):
            at = i * NB - start[k]
            change = times(right[:, at : at + NB], left, over_rows)
            behind[i] = -change if behind[i] is None else widen(behind[i], reach) - change
    basis = times(scaled, jnp.concatenate(inverse, 0), (((1,), (1,)), ((), ())))
    basis_ref[...] = basis.astype(BF16)


def factor_and_basis(mine, other, second, scale_root):
    rows, size = second.shape
    return pl.pallas_call(
        functools.partial(factor_kernel, scale_root),
        out_shape=(
            jax.ShapeDtypeStruct((rows, size), BF16),
            jax.ShapeDtypeStruct((size, size), F32),
        ),
        in_specs=[VMEM] * 3,
        out_specs=(VMEM, VMEM),
        scratch_shapes=[
            pltpu.VMEM((size + 16, size // 2), F32),
        ],
        name="factor_kernel",
        compiler_params=pltpu.CompilerParams(vmem_limit_bytes=16 << 20),
    )(mine, other, second)


def halo_step(send, swapped):
    slabs, bands = lax.axis_size("rows"), lax.axis_size("band")
    pairs = []
    for r in range(slabs):
        for b in range(bands):
            source = r - 1 if b < bands // 2 else r + 1
            if 0 <= source < slabs:
                pairs.append((source * bands + (b ^ 2 if swapped else b), r * bands + b))
    return lax.ppermute(send, ("rows", "band"), pairs)


def inner_step(halo):
    return flip(halo, "band", 1)


def doubling_steps(slabs, bands):
    levels = [2] + [bit * bands for bit in (1 << i for i in range(slabs.bit_length() - 1))]
    turn = len(levels) // 2
    orders = (levels, levels[turn:] + levels[:turn])
    return [
        [(d, d ^ orders[d % 2][step]) for d in range(slabs * bands)] for step in range(len(levels))
    ]


def add16(*parts):
    total = parts[0].astype(F32)
    for part in parts[1:]:
        total = total + part.astype(F32)
    return total.astype(BF16)


def per_device(coupling, sketch):
    slabs = lax.axis_size("rows")
    scale_root = math.sqrt(sketch.shape[0] * slabs)

    halo = halo_step(edge_of(sketch), False)
    keep, send, coupling, sketch = product(first_kernel, coupling, sketch)
    near = flip(send, "band", 1)
    far = flip(add16(keep, near), "band", 2)
    halo2 = inner_step(halo)
    keep, send = product(late_kernel_slab, coupling, sketch, halo, halo2)
    own = add16(keep, flip(send, "band", 1), far)

    across = flip(own, "band", 2)
    halo = halo_step(across, False)
    own2 = flip(own, "band", 1)
    across2 = flip(across, "band", 1)
    keep, send = product(early_kernel, coupling, own, own2, across, across2)
    near = flip(send, "band", 1)
    far = flip(add16(keep, near), "band", 2)
    halo2 = inner_step(halo)
    keep, send = product(late_kernel, coupling, own, own2, halo, halo2)
    near = flip(send, "band", 1)

    second, mine, other = gram(keep, near, far)
    mine = mine + flip(other, "band", 1)
    for pairs in doubling_steps(slabs, lax.axis_size("band")):
        mine = mine + lax.ppermute(mine, ("rows", "band"), pairs)
    other = flip(mine, "band", 1)
    return factor_and_basis(mine, other, second, scale_root)


def solution(mesh):
    in_specs = (P("rows", "band"), P("rows", None))
    out_specs = (P(("rows", "band"), None), P())

    return jax.shard_map(
        per_device, mesh=mesh, in_specs=in_specs, out_specs=out_specs, check_vma=False
    )
```
